32 devices in a mesh: prow: 8 (over y, x, core), pcol: 4 (over z).
Axes of the slice: x: 2, y: 2, z: 4, core: 2. Of those that a mesh axis runs over, the one named last changes fastest.
Arguments:
- panel: float32 [16, 1024, 128], P('pcol', 'prow'), may hold values from -8 to 192, as said below
- strip: float32 [16, 1024, 2, 512], P(None, 'prow', None, 'pcol'), may hold values from -6 to 6
- factor: float32 [16, 1024, 2, 512], P(None, 'prow', None, 'pcol'), may hold values from -0.125 to 0.125
- inv_diag: float32 [8, 128, 128], replicated, may hold values from -0.24 to 1.4, as said below
- rhs: float32 [16, 1024, 256], P(None, 'prow'), may hold values from -6 to 6
Outputs:
- panel_factor: float32 [16, 1024, 128], P('pcol', 'prow')
- new_strip: float32 [16, 1024, 2, 512], P(None, 'prow', None, 'pcol')
- forward: float32 [16, 1024, 256], P(None, 'prow')
The draws below stay inside these ranges and needn't reach their ends.
Inputs may be any that keep to these rules, and one draw needn't show every extreme that they name: Row tile 8 of the panel, read as in the first step, is symmetric positive definite. `inv_diag`: every block is lower triangular with a positive diagonal.
All inputs are finite; a program needn't handle non-finite values.
Results may differ from the reference program's by a relative error of at most 0.00018.
Values sent between devices are 32-bit elements; how exact they have to be, the bound alone decides.
A program may use at most 64 MiB of HBM per device.

```python
import jax
import jax.numpy as jnp
from jax import lax

TILE = 128
TPD = 16
KF = 2
CTD = 2
NRHS = 256
NROWS = 16384
KSWEEP = 8
KSTRIP = 8
N_PROW = 8
N_PCOL = 4


def draw_panel(key, part):
    key_base, key_points, key_nugget = jax.random.split(key, 3)
    base = jax.random.truncated_normal(key_base, -4.0, 4.0, (NROWS, TILE), jnp.float32) * 2.0
    points = jax.random.uniform(key_points, (TILE, 1, 3), jnp.float32, 0.0, 1.0)
    distance = jnp.sum(jnp.abs(points - jnp.transpose(points, (1, 0, 2))), axis=2)
    kernel = jnp.exp(-distance / 0.5)
    nugget = jax.random.uniform(key_nugget, (TILE,), jnp.float32, 0.5, 2.0)
    unit = jnp.eye(TILE, dtype=jnp.float32)
    block = 64.0 * (kernel + unit * nugget[None, :])
    whole = lax.dynamic_update_slice(base, block, (KSWEEP * TILE, 0))
    return whole.reshape(TPD, NROWS // TPD, TILE)


def draw_inv_diag(key, part):
    key_off, key_diag = jax.random.split(key, 2)
    off_part = jax.random.truncated_normal(key_off, -3.0, 3.0, (KSWEEP, TILE, TILE), jnp.float32) * 0.08
    diag_values = jax.random.uniform(key_diag, (KSWEEP, TILE, 1), jnp.float32, 0.6, 1.4)
    strict_lower = jnp.tril(jnp.ones((TILE, TILE), jnp.float32), -1)
    unit = jnp.eye(TILE, dtype=jnp.float32)
    return off_part * strict_lower[None] + unit[None] * diag_values


def levels(key, dims, shards, low, largest):
    gain = 1.0
    for position, parts in shards:
        steps = jax.random.uniform(jax.random.fold_in(jax.random.fold_in(key, 6), position), (parts,), jnp.float32, low / len(shards), largest / len(shards))
        gain = gain * jnp.repeat(jnp.exp(steps), dims[position] // parts).reshape((-1,) + (1,) * (len(dims) - 1 - position))
    return gain


def bell_draw(own_key, shape, width, most, cuts=(), kind=jnp.bfloat16):
    result = width * jax.random.normal(own_key, shape, jnp.float32)
    if cuts:
        result = result * levels(own_key, shape, cuts, -0.22, 0.18)
    return jnp.clip(result, -most, most).astype(kind)


def setup_inputs(seed: int = 0) -> dict:
    splits = jax.random.split(jax.random.key(seed), 6)
    return {
        "panel": draw_panel(jax.random.fold_in(splits[5], 71), 0),
        "strip": bell_draw(splits[1], (TPD, N_PROW * TILE, CTD, N_PCOL * TILE), 1.0, 6.0, ((1, 8), (3, 4)), jnp.float32),
        "factor": bell_draw(splits[2], (TPD, N_PROW * TILE, KF, N_PCOL * TILE), (16 * TILE) ** -0.5, 0.125, ((1, 8), (3, 4)), jnp.float32),
        "inv_diag": draw_inv_diag(jax.random.fold_in(splits[5], 71), 0),
        "rhs": bell_draw(splits[4], (TPD, N_PROW * TILE, NRHS), 1.0, 6.0, ((1, 8),), jnp.float32),
    }


def reference(panel, strip, factor, inv_diag, rhs):
    highest = lax.Precision.HIGHEST
    panel_mat = panel.reshape(NROWS, TILE)
    strip_mat = strip.reshape(NROWS, KSTRIP * TILE)
    factor_mat = factor.reshape(NROWS, KSWEEP * TILE)
    rhs_mat = rhs.reshape(NROWS, NRHS)
    diag_block = panel_mat[KSWEEP * TILE:(KSWEEP + 1) * TILE]
    diag_factor = jnp.linalg.cholesky(diag_block)
    inverse = jax.scipy.linalg.solve_triangular(diag_factor, jnp.eye(TILE, dtype=diag_block.dtype), lower=True)
    scaled = jnp.dot(panel_mat, inverse.T, precision=highest)
    tile_index = jnp.arange(NROWS) // TILE
    below_part = jnp.where((tile_index > KSWEEP)[:, None], scaled, 0.0)
    panel_out = below_part.at[KSWEEP * TILE:(KSWEEP + 1) * TILE].set(diag_factor)
    column = below_part[(KSWEEP + 1) * TILE:(KSWEEP + 1 + KSTRIP) * TILE]
    strip_out = strip_mat - jnp.dot(below_part, column.T, precision=highest)
    solved = []
    for sweep_step in range(KSWEEP):
        residue = rhs_mat[sweep_step * TILE:(sweep_step + 1) * TILE]
        if sweep_step > 0:
            earlier = jnp.concatenate(solved, axis=0)
            block_row = factor_mat[sweep_step * TILE:(sweep_step + 1) * TILE, :sweep_step * TILE]
            residue = residue - jnp.dot(block_row, earlier, precision=highest)
        solved.append(jnp.dot(inv_diag[sweep_step], residue, precision=highest))
    stacked = jnp.concatenate(solved, axis=0)
    remains = rhs_mat - jnp.dot(factor_mat, stacked, precision=highest)
    panel_solution = jnp.dot(inverse, remains[KSWEEP * TILE:(KSWEEP + 1) * TILE], precision=highest)
    remains = remains - jnp.dot(below_part, panel_solution, precision=highest)
    remains = remains.at[:KSWEEP * TILE].set(stacked)
    remains = remains.at[KSWEEP * TILE:(KSWEEP + 1) * TILE].set(panel_solution)
    return (panel_out.reshape(panel.shape), strip_out.reshape(strip.shape), remains.reshape(rhs.shape))
```

```python
import functools

import jax
import jax.numpy as jnp
from jax import lax
from jax.experimental import pallas as pl
from jax.experimental.pallas import tpu as pltpu
from jax.sharding import PartitionSpec as P

HIGHEST = lax.Precision.HIGHEST
MESH = pl.DeviceIdType.MESH


def dot(a, b):
    return jnp.dot(a, b, precision=HIGHEST, preferred_element_type=jnp.float32)


def when(cond, body):
    if cond is True:
        body()
    else:
        pl.when(cond)(body)


def kernel(
    R, C,
    panel, strip, factor, inv_diag, rhs,
    panel_out, strip_out, forward,
    pan_all, diag, col, ftri, brow, y, frow, tri, inv, inv_t,
    z_send, z_recv, p_send, p_recv, a_send, a_recv, local_sem,
):
    r = lax.axis_index("prow")
    c = lax.axis_index("pcol")
    A, TILE, _ = panel.shape
    KF = factor.shape[0]
    CTD = strip.shape[0]
    I = factor.shape[1]
    KS = KF * C
    NR = rhs.shape[2]
    full = KS == R

    def target(row):
        return jnp.where(row == 0, KS, row) if full else row

    def has_row(row):
        return True if full else jnp.logical_and(row >= 1, row <= KS)

    def slot(row):
        return target(row) if full else jnp.minimum(row, KS)

    first = jnp.where(r == 0, KS // R, 0) if full else 0

    barrier = pltpu.get_barrier_semaphore()

    @pl.loop(1, C)
    def _(d):
        pl.semaphore_signal(barrier, inc=1, device_id={"pcol": lax.rem(c + d, C)}, device_id_type=MESH)

    @pl.loop(1, R)
    def _(d):
        pl.semaphore_signal(barrier, inc=1, device_id={"prow": lax.rem(r + d, R)}, device_id_type=MESH)

    pl.semaphore_wait(barrier, C - 1 + R - 1)

    def z_copy(kind, d, source, place):
        if kind == 0:
            src, dst = factor.at[:, first], ftri.at[slot(r), :, source]
        elif kind == 1:
            src, dst = panel, pan_all.at[pl.ds(source * A, A)]
        else:
            src, dst = factor.at[:, pl.ds(place * A, A)], frow.at[:, source]
        return pltpu.make_async_remote_copy(
            src_ref=src, dst_ref=dst, send_sem=z_send.at[kind, d - 1], recv_sem=z_recv.at[kind, d - 1],
            device_id={"pcol": place}, device_id_type=MESH,
        )

    def z_cond(kind):
        return has_row(r) if kind == 0 else True

    def z_each(kind, act):
        for d in range(1, C):
            when(z_cond(kind), lambda d=d: act(d))

    def z_start(kind):
        z_each(kind, lambda d: z_copy(kind, d, c, lax.rem(c + d, C)).start())

    def z_wait_send(kind):
        z_each(kind, lambda d: z_copy(kind, d, c, lax.rem(c + d, C)).wait_send())

    def z_wait_recv(kind):
        z_each(kind, lambda d: z_copy(kind, d, lax.rem(c + C - d, C), c).wait_recv())

    def wanted(s):
        return KS + 1 + s * C + c

    def p_copy(kind, d, row):
        if kind == 0:
            src, dst = rhs.at[0], brow.at[jnp.minimum(row, KS - 1)]
        elif kind == 1:
            src, dst = rhs.at[KS // R], brow.at[KS]
        elif kind == 2:
            src, dst = pan_all.at[KS // R], diag
        elif kind < 3 + CTD:
            s = kind - 3
            src, dst = pan_all.at[wanted(s) // R], col.at[s]
        else:
            s = kind - 3 - CTD
            src, dst = ftri.at[slot(row), s], ftri.at[slot(row), s]
        return pltpu.make_async_remote_copy(
            src_ref=src, dst_ref=dst, send_sem=p_send.at[kind, d - 1], recv_sem=p_recv.at[kind, d - 1],
            device_id={"prow": lax.rem(r + d, R)}, device_id_type=MESH,
        )

    def p_cond(kind, row):
        if kind == 0:
            return True if full else row < KS
        if kind <= 2:
            return row == KS % R
        if kind < 3 + CTD:
            return row == lax.rem(wanted(kind - 3), R)
        s = kind - 3 - CTD
        if full and s == 0:
            return True
        deep = target(row) > s * C
        return deep if full else jnp.logical_and(deep, row <= KS)

    def p_start(kinds):
        @pl.loop(1, R)
        def _(d):
            for kind in kinds:
                when(p_cond(kind, r), lambda kind=kind: p_copy(kind, d, r).start())

    def p_wait_send(kinds):
        @pl.loop(1, R)
        def _(d):
            for kind in kinds:
                when(p_cond(kind, r), lambda kind=kind: p_copy(kind, d, r).wait_send())

    def p_wait_recv(kinds):
        @pl.loop(1, R)
        def _(d):
            row = lax.rem(r + R - d, R)
            for kind in kinds:
                when(p_cond(kind, row), lambda kind=kind: p_copy(kind, d, row).wait_recv())

    row_kinds = tuple(range(3 + CTD, 3 + CTD + KF))

    z_start(0)
    p_start((0, 1))
    z_start(1)
    z_start(2)

    own = pltpu.make_async_copy(factor.at[:, pl.ds(c * A, A)], frow.at[:, c], local_sem)
    own.start()

    def keep_row():
        ftri[slot(r), :, c] = factor[:, first]

    when(has_row(r), keep_row)
    pan_all[pl.ds(c * A, A)] = panel[...]

    def keep_rhs():
        brow[jnp.minimum(r, KS - 1)] = rhs[0]

    when(p_cond(0, r), keep_rhs)

    @pl.when(p_cond(1, r))
    def _():
        brow[KS] = rhs[KS // R]

    z_wait_recv(0)
    p_start(row_kinds)
    z_wait_recv(1)
    p_start(tuple(range(2, 3 + CTD)))

    @pl.when(p_cond(2, r))
    def _():
        diag[...] = pan_all[KS // R]

    for s in range(CTD):
        @pl.when(p_cond(3 + s, r))
        def _(s=s):
            col[s] = pan_all[wanted(s) // R]

    p_wait_recv((2,))
    lanes = lax.broadcasted_iota(jnp.int32, (TILE, TILE), 1)
    rows = lax.broadcasted_iota(jnp.int32, (TILE, TILE), 0)
    tri[...] = diag[...]
    inv[...] = jnp.where(lanes == rows, 1.0, 0.0)

    def eliminate(k, carry):
        lane = lanes[0:1]
        row = tri[pl.ds(k, 1), :]
        whole = tri[...]
        pivot = jnp.sum(jnp.where(lane == k, row, 0.0), axis=1, keepdims=True)
        scale = 1.0 / jnp.sqrt(pivot)
        lrow = jnp.where(lane >= k, row * scale, 0.0)
        column = jnp.sum(jnp.where(lanes == k, whole, 0.0), axis=1, keepdims=True)
        lcol = jnp.where(rows[:, 0:1] > k, column * scale, 0.0)
        wrow = inv[pl.ds(k, 1), :] * scale
        tri[...] = whole - lcol * lrow
        inv[...] = inv[...] - lcol * wrow
        tri[pl.ds(k, 1), :] = lrow
        inv[pl.ds(k, 1), :] = wrow
        return carry

    lax.fori_loop(0, TILE, eliminate, 0)
    inv_t[...] = inv[...].T

    p_wait_recv((0, 1) + row_kinds)

    def advance(t, carry):
        y[t] = dot(inv_diag[t], brow[t])

        def update(row, carry):
            brow[row] = brow[row] - dot(ftri[row, t // C, lax.rem(t, C)], y[t])
            return carry

        return lax.fori_loop(t + 1, KS + 1, update, carry)

    lax.fori_loop(0, KS, advance, 0)
    panel_solution = dot(inv[...], brow[KS])

    scaled = dot(panel[...].reshape(A * TILE, TILE), inv_t[...])
    for a in range(A):
        tile = (c * A + a) * R + r
        panel_out[a] = jnp.where(tile > KS, scaled[a * TILE:(a + 1) * TILE], 0.0)
    brow[KS] = panel_solution

    z_wait_recv(2)
    own.wait()

    mine = pl.ds(c * A, A)
    below = panel_out[...].reshape(A * TILE, TILE)
    forward[mine] = rhs[mine] - dot(below, brow[KS]).reshape(A, TILE, NR)

    def reach(j, carry):
        part = dot(frow[j // C, lax.rem(j, C)].reshape(A * TILE, TILE), y[j])
        forward[mine] = forward[mine] - part.reshape(A, TILE, NR)
        return carry

    lax.fori_loop(0, KS, reach, 0)

    def settle(a, carry):
        tile = (c * A + a) * R + r

        @pl.when(tile < KS)
        def _():
            forward[c * A + a] = y[jnp.minimum(tile, KS - 1)]

        @pl.when(tile == KS)
        def _():
            forward[c * A + a] = brow[KS]
            panel_out[a] = tri[...].T

        return carry

    lax.fori_loop(0, A, settle, 0)

    def a_copy(d, source, place):
        span = pl.ds(source * A, A)
        return pltpu.make_async_remote_copy(
            src_ref=forward.at[span], dst_ref=forward.at[span],
            send_sem=a_send.at[d - 1], recv_sem=a_recv.at[d - 1],
            device_id={"pcol": place}, device_id_type=MESH,
        )

    for d in range(1, C):
        a_copy(d, c, lax.rem(c + d, C)).start()

    p_wait_recv(tuple(range(3, 3 + CTD)))
    for s in range(CTD):
        col[s] = dot(col[s], inv_t[...]).T

    def strip_row(i, carry):
        tile = i * R + r
        scaled = jnp.where(tile > KS, dot(pan_all[i], inv_t[...]), 0.0)
        for s in range(CTD):
            strip_out[s, i] = strip[s, i] - dot(scaled, col[s])
        return carry

    lax.fori_loop(0, I, strip_row, 0)

    for kind in range(3):
        z_wait_send(kind)
    p_wait_send(tuple(range(3 + CTD + KF)))
    for d in range(1, C):
        a_copy(d, lax.rem(c + C - d, C), c).wait_recv()
    for d in range(1, C):
        a_copy(d, c, lax.rem(c + d, C)).wait_send()


def per_device(panel, strip, factor, inv_diag, rhs):
    R = lax.axis_size("prow")
    C = lax.axis_size("pcol")
    A, TILE, _ = panel.shape
    I, _, CTD, _ = strip.shape
    KF = factor.shape[2]
    NR = rhs.shape[2]
    KS = KF * C
    assert KS <= R
    f32 = jnp.float32
    strip = jnp.transpose(strip, (2, 0, 1, 3))
    factor = jnp.transpose(factor, (2, 0, 1, 3))
    kinds = 3 + CTD + KF
    dma = pltpu.SemaphoreType.DMA
    panel_factor, new_strip, forward = pl.pallas_call(
        functools.partial(kernel, R, C),
        out_shape=(
            jax.ShapeDtypeStruct(panel.shape, f32),
            jax.ShapeDtypeStruct(strip.shape, f32),
            jax.ShapeDtypeStruct(rhs.shape, f32),
        ),
        in_specs=[pl.BlockSpec(memory_space=pltpu.VMEM)] * 5,
        out_specs=[pl.BlockSpec(memory_space=pltpu.VMEM)] * 3,
        scratch_shapes=[
            pltpu.VMEM((I, TILE, TILE), f32),
            pltpu.VMEM((TILE, TILE), f32),
            pltpu.VMEM((CTD, TILE, TILE), f32),
            pltpu.VMEM((KS + 1, KF, C, TILE, TILE), f32),
            pltpu.VMEM((KS + 1, TILE, NR), f32),
            pltpu.VMEM((KS, TILE, NR), f32),
            pltpu.VMEM((KF, C, A, TILE, TILE), f32),
            pltpu.VMEM((TILE, TILE), f32),
            pltpu.VMEM((TILE, TILE), f32),
            pltpu.VMEM((TILE, TILE), f32),
            dma((3, C - 1)),
            dma((3, C - 1)),
            dma((kinds, R - 1)),
            dma((kinds, R - 1)),
            dma((C - 1,)),
            dma((C - 1,)),
            dma,
        ],
        compiler_params=pltpu.CompilerParams(
            collective_id=0, has_side_effects=True, vmem_limit_bytes=56 << 20
        ),
    )(panel, strip, factor, inv_diag, rhs)
    return panel_factor, jnp.transpose(new_strip, (1, 2, 0, 3)), forward


def solution(mesh):
    in_specs = (
        P("pcol", "prow", None),
        P(None, "prow", None, "pcol"),
        P(None, "prow", None, "pcol"),
        P(),
        P(None, "prow", None),
    )
    out_specs = (P("pcol", "prow", None), P(None, "prow", None, "pcol"), P(None, "prow", None))
    return jax.shard_map(
        per_device, mesh=mesh, in_specs=in_specs, out_specs=out_specs, check_vma=False
    )
```

```python
import functools

import jax
import jax.numpy as jnp
from jax import lax
from jax.experimental import pallas as pl
from jax.experimental.pallas import tpu as pltpu
from jax.sharding import PartitionSpec as P

HIGHEST = lax.Precision.HIGHEST
MESH = pl.DeviceIdType.MESH


def dot(a, b):
    return jnp.dot(a, b, precision=HIGHEST, preferred_element_type=jnp.float32)


def when(cond, body):
    if cond is True:
        body()
    else:
        pl.when(cond)(body)


def kernel(
    R, C,
    panel, strip, factor, inv_diag, rhs,
    panel_out, strip_out, forward,
    pan_all, diag, col, ftri, brow, y, frow, tri, inv, inv_t,
    z_send, z_recv, p_send, p_recv, f_send, a_send, a_recv, local_sem,
):
    r = lax.axis_index("prow")
    c = lax.axis_index("pcol")
    A, TILE, _ = panel.shape
    KF = factor.shape[0]
    CTD = strip.shape[0]
    I = factor.shape[1]
    KS = KF * C
    NR = rhs.shape[2]
    full = KS == R

    def target(row):
        return jnp.where(row == 0, KS, row) if full else row

    def has_row(row):
        return True if full else jnp.logical_and(row >= 1, row <= KS)

    def slot(row):
        return target(row) if full else jnp.minimum(row, KS)

    first = jnp.where(r == 0, KS // R, 0) if full else 0

    barrier = pltpu.get_barrier_semaphore()

    @pl.loop(1, C)
    def _(d):
        pl.semaphore_signal(barrier, inc=1, device_id={"pcol": lax.rem(c + d, C)}, device_id_type=MESH)

    @pl.loop(1, R)
    def _(d):
        pl.semaphore_signal(barrier, inc=1, device_id={"prow": lax.rem(r + d, R)}, device_id_type=MESH)

    pl.semaphore_wait(barrier, C - 1 + R - 1)

    def z_copy(kind, d, source, place):
        if kind < KF:
            src, dst = factor.at[kind, first], ftri.at[slot(r), kind * C + source]
        elif kind == KF:
            src, dst = panel, pan_all.at[pl.ds(source * A, A)]
        else:
            src, dst = factor.at[:, pl.ds(place * A, A)], frow.at[:, source]
        return pltpu.make_async_remote_copy(
            src_ref=src, dst_ref=dst, send_sem=z_send.at[kind, d - 1], recv_sem=z_recv.at[kind, d - 1],
            device_id={"pcol": place}, device_id_type=MESH,
        )

    def tiles_of(row):
        return target(row) if full else jnp.where(row <= KS, row, 0)

    def z_cond(kind, source):
        return kind * C + source < tiles_of(r) if kind < KF else True

    def z_start(kind):
        for d in range(1, C):
            when(z_cond(kind, c), lambda d=d: z_copy(kind, d, c, lax.rem(c + d, C)).start())

    def z_wait_send(kind):
        for d in range(1, C):
            when(z_cond(kind, c), lambda d=d: z_copy(kind, d, c, lax.rem(c + d, C)).wait_send())

    def z_wait_recv(kind):
        for d in range(1, C):
            source = lax.rem(c + C - d, C)
            when(z_cond(kind, source), lambda d=d, source=source: z_copy(kind, d, source, c).wait_recv())

    side = lax.rem(r, 2)
    sibling = r + 1 - 2 * side

    def wanted(s):
        return KS + 1 + s * C + c

    def p_place(kind, row):
        if kind == 0:
            return brow.at[jnp.minimum(row, KS - 1)]
        if kind == 1:
            return brow.at[KS]
        if kind == 2:
            return diag
        return col.at[kind - 3]

    def p_cond(kind, row):
        if kind == 0:
            return True if full else row < KS
        if kind <= 2:
            return row == KS % R
        return row == lax.rem(wanted(kind - 3), R)

    def p_copy(kind, row, place, sem):
        ref = p_place(kind, row)
        return pltpu.make_async_remote_copy(
            src_ref=ref, dst_ref=ref, send_sem=sem, recv_sem=p_recv.at[kind, row],
            device_id={"prow": place}, device_id_type=MESH,
        )

    def t_copy(j, row, place, sem):
        ref = ftri.at[slot(row), j]
        return pltpu.make_async_remote_copy(
            src_ref=ref, dst_ref=ref, send_sem=sem, recv_sem=p_recv.at[3 + CTD + j, row],
            device_id={"prow": place}, device_id_type=MESH,
        )

    def each(kinds, row, act, t_act):
        for kind in kinds:
            if kind == "tiles":
                def one(j, carry):
                    t_act(j)
                    return carry

                lax.fori_loop(0, tiles_of(row), one, 0)
            else:
                when(p_cond(kind, row), lambda kind=kind: act(kind))

    def p_own(kinds, finish):
        def go(copy):
            if finish:
                copy.wait_send()
            else:
                copy.start()

        @pl.loop(0, R // 2)
        def _(d):
            place = jnp.where(d == 0, sibling, lax.rem(r + 2 * d, R))
            each(
                kinds, r,
                lambda kind: go(p_copy(kind, r, place, p_send.at[kind, d])),
                lambda j: go(t_copy(j, r, place, p_send.at[3 + CTD + j, d])),
            )

    def p_pass(kinds):
        @pl.loop(1, R // 2)
        def _(d):
            row = lax.rem(r + R - 2 * d, R)

            def act(kind):
                p_copy(kind, row, sibling, f_send.at[kind, d]).wait_recv()
                p_copy(kind, row, sibling, f_send.at[kind, d]).start()

            def t_act(j):
                t_copy(j, row, sibling, f_send.at[3 + CTD + j, d]).wait_recv()
                t_copy(j, row, sibling, f_send.at[3 + CTD + j, d]).start()

            each(kinds, row, act, t_act)

    def p_pass_done(kinds):
        @pl.loop(1, R // 2)
        def _(d):
            row = lax.rem(r + R - 2 * d, R)
            each(
                kinds, row,
                lambda kind: p_copy(kind, row, sibling, f_send.at[kind, d]).wait_send(),
                lambda j: t_copy(j, row, sibling, f_send.at[3 + CTD + j, d]).wait_send(),
            )

    def p_rest(kinds):
        @pl.loop(0, R // 2)
        def _(d):
            row = 2 * d + 1 - side
            each(
                kinds, row,
                lambda kind: p_copy(kind, row, sibling, f_send.at[kind, 0]).wait_recv(),
                lambda j: t_copy(j, row, sibling, f_send.at[3 + CTD + j, 0]).wait_recv(),
            )

    for kind in range(KF):
        z_start(kind)

    own = pltpu.make_async_copy(factor.at[:, pl.ds(c * A, A)], frow.at[:, c], local_sem)
    own.start()

    def keep_rhs():
        brow[jnp.minimum(r, KS - 1)] = rhs[0]

    when(p_cond(0, r), keep_rhs)

    @pl.when(p_cond(1, r))
    def _():
        brow[KS] = rhs[KS // R]

    for s in range(KF):
        @pl.when(z_cond(s, c))
        def _(s=s):
            ftri[slot(r), s * C + c] = factor[s, first]

    pan_all[pl.ds(c * A, A)] = panel[...]
    for kind in range(KF):
        z_wait_recv(kind)
    z_start(KF)
    p_own(("tiles", 0, 1), False)
    z_wait_recv(KF)
    z_start(KF + 1)

    @pl.when(p_cond(2, r))
    def _():
        diag[...] = pan_all[KS // R]

    for s in range(CTD):
        @pl.when(p_cond(3 + s, r))
        def _(s=s):
            col[s] = pan_all[wanted(s) // R]

    late = tuple(range(2, 3 + CTD))
    p_own(late, False)
    p_pass(("tiles", 0, 1) + late)
    p_rest(late)

    lanes = lax.broadcasted_iota(jnp.int32, (TILE, TILE), 1)
    rows = lax.broadcasted_iota(jnp.int32, (TILE, TILE), 0)
    tri[...] = diag[...]
    inv[...] = jnp.where(lanes == rows, 1.0, 0.0)

    def eliminate(k, carry):
        lane = lanes[0:1]
        row = tri[pl.ds(k, 1), :]
        whole = tri[...]
        pivot = jnp.sum(jnp.where(lane == k, row, 0.0), axis=1, keepdims=True)
        scale = 1.0 / jnp.sqrt(pivot)
        lrow = jnp.where(lane >= k, row * scale, 0.0)
        column = jnp.sum(jnp.where(lanes == k, whole, 0.0), axis=1, keepdims=True)
        lcol = jnp.where(rows[:, 0:1] > k, column * scale, 0.0)
        wrow = inv[pl.ds(k, 1), :] * scale
        tri[...] = whole - lcol * lrow
        inv[...] = inv[...] - lcol * wrow
        tri[pl.ds(k, 1), :] = lrow
        inv[pl.ds(k, 1), :] = wrow
        return carry

    lax.fori_loop(0, TILE, eliminate, 0)
    inv_t[...] = inv[...].T

    p_rest(("tiles", 0, 1))
    p_own((0, 1), True)
    p_pass_done((0, 1))

    def advance(t, carry):
        y[t] = dot(inv_diag[t], brow[t])

        def update(row, carry):
            brow[row] = brow[row] - dot(ftri[row, t], y[t])
            return carry

        return lax.fori_loop(t + 1, KS + 1, update, carry)

    lax.fori_loop(0, KS, advance, 0)
    panel_solution = dot(inv[...], brow[KS])

    scaled = dot(panel[...].reshape(A * TILE, TILE), inv_t[...])
    for a in range(A):
        tile = (c * A + a) * R + r
        panel_out[a] = jnp.where(tile > KS, scaled[a * TILE:(a + 1) * TILE], 0.0)
    brow[KS] = panel_solution

    z_wait_recv(KF + 1)
    own.wait()

    def a_copy(way, source, a):
        place = jnp.clip(c + (1 if way else -1), 0, C - 1)
        ref = forward.at[source * A + a]
        return pltpu.make_async_remote_copy(
            src_ref=ref, dst_ref=ref,
            send_sem=a_send.at[way, source, a], recv_sem=a_recv.at[source, a],
            device_id={"pcol": place}, device_id_type=MESH,
        )

    p_own(late, True)
    p_pass_done(late)
    for s in range(CTD):
        col[s] = dot(col[s], inv_t[...]).T

    def finish(a, carry):
        tile = (c * A + a) * R + r
        total = rhs[c * A + a] - dot(panel_out[a], brow[KS])

        def reach(j, total):
            return total - dot(frow[j // C, lax.rem(j, C), a], y[j])

        total = lax.fori_loop(0, KS, reach, total, unroll=True)
        forward[c * A + a] = total

        @pl.when(tile < KS)
        def _():
            forward[c * A + a] = y[jnp.minimum(tile, KS - 1)]

        @pl.when(tile == KS)
        def _():
            forward[c * A + a] = brow[KS]
            panel_out[a] = tri[...].T

        @pl.when(c < C - 1)
        def _():
            a_copy(1, c, a).start()

        @pl.when(c > 0)
        def _():
            a_copy(0, c, a).start()

        return carry

    lax.fori_loop(0, A, finish, 0)

    def strip_row(i, carry):
        tile = i * R + r
        scaled = jnp.where(tile > KS, dot(pan_all[i], inv_t[...]), 0.0)
        for s in range(CTD):
            strip_out[s, i] = strip[s, i] - dot(scaled, col[s])
        return carry

    steps = (C - 1) * A

    def hop(n, carry):
        lax.fori_loop(n * I // steps, (n + 1) * I // steps, strip_row, 0)
        far = n // A + 1
        a = lax.rem(n, A)

        @pl.when(c - far >= 0)
        def _():
            a_copy(1, c - far, a).wait_recv()

            @pl.when(c < C - 1)
            def _():
                a_copy(1, c - far, a).start()

        @pl.when(c + far < C)
        def _():
            a_copy(0, c + far, a).wait_recv()

            @pl.when(c > 0)
            def _():
                a_copy(0, c + far, a).start()

        return carry

    lax.fori_loop(0, steps, hop, 0)

    for kind in range(KF + 2):
        z_wait_send(kind)
    p_own(("tiles",), True)
    p_pass_done(("tiles",))

    def flush(n, carry):
        source = n // A
        a = lax.rem(n, A)

        @pl.when(jnp.logical_and(source <= c, c < C - 1))
        def _():
            a_copy(1, source, a).wait_send()

        @pl.when(jnp.logical_and(source >= c, c > 0))
        def _():
            a_copy(0, source, a).wait_send()

        return carry

    lax.fori_loop(0, C * A, flush, 0)


def per_device(panel, strip, factor, inv_diag, rhs):
    R = lax.axis_size("prow")
    C = lax.axis_size("pcol")
    A, TILE, _ = panel.shape
    I, _, CTD, _ = strip.shape
    KF = factor.shape[2]
    NR = rhs.shape[2]
    KS = KF * C
    assert KS <= R
    f32 = jnp.float32
    strip = jnp.transpose(strip, (2, 0, 1, 3))
    factor = jnp.transpose(factor, (2, 0, 1, 3))
    kinds = 3 + CTD + KS
    dma = pltpu.SemaphoreType.DMA
    panel_factor, new_strip, forward = pl.pallas_call(
        functools.partial(kernel, R, C),
        out_shape=(
            jax.ShapeDtypeStruct(panel.shape, f32),
            jax.ShapeDtypeStruct(strip.shape, f32),
            jax.ShapeDtypeStruct(rhs.shape, f32),
        ),
        in_specs=[pl.BlockSpec(memory_space=pltpu.VMEM)] * 5,
        out_specs=[pl.BlockSpec(memory_space=pltpu.VMEM)] * 3,
        scratch_shapes=[
            pltpu.VMEM((I, TILE, TILE), f32),
            pltpu.VMEM((TILE, TILE), f32),
            pltpu.VMEM((CTD, TILE, TILE), f32),
            pltpu.VMEM((KS + 1, KS, TILE, TILE), f32),
            pltpu.VMEM((KS + 1, TILE, NR), f32),
            pltpu.VMEM((KS, TILE, NR), f32),
            pltpu.VMEM((KF, C, A, TILE, TILE), f32),
            pltpu.VMEM((TILE, TILE), f32),
            pltpu.VMEM((TILE, TILE), f32),
            pltpu.VMEM((TILE, TILE), f32),
            dma((KF + 2, C - 1)),
            dma((KF + 2, C - 1)),
            dma((kinds, R // 2)),
            dma((kinds, R)),
            dma((kinds, R // 2)),
            dma((2, C, A)),
            dma((C, A)),
            dma,
        ],
        compiler_params=pltpu.CompilerParams(
            collective_id=0, has_side_effects=True, vmem_limit_bytes=56 << 20
        ),
    )(panel, strip, factor, inv_diag, rhs)
    return panel_factor, jnp.transpose(new_strip, (1, 2, 0, 3)), forward


def solution(mesh):
    in_specs = (
        P("pcol", "prow", None),
        P(None, "prow", None, "pcol"),
        P(None, "prow", None, "pcol"),
        P(),
        P(None, "prow", None),
    )
    out_specs = (P("pcol", "prow", None), P(None, "prow", None, "pcol"), P(None, "prow", None))
    return jax.shard_map(
        per_device, mesh=mesh, in_specs=in_specs, out_specs=out_specs, check_vma=False
    )
```

```python
import functools

import jax
import jax.numpy as jnp
from jax import lax
from jax.experimental import pallas as pl
from jax.experimental.pallas import tpu as pltpu
from jax.sharding import PartitionSpec as P

HIGHEST = lax.Precision.HIGHEST
MESH = pl.DeviceIdType.MESH


def dot(a, b):
    return jnp.dot(a, b, precision=HIGHEST, preferred_element_type=jnp.float32)


def when(cond, body):
    if cond is True:
        body()
    else:
        pl.when(cond)(body)


def kernel(
    R, C,
    panel, strip, factor, inv_diag, rhs,
    panel_out, strip_out, forward,
    pan_all, diag, col, ftri, brow, y, frow, tri, inv, inv_t,
    z_send, z_recv, p_send, p_recv, f_send, a_send, a_recv, local_sem,
):
    r = lax.axis_index("prow")
    c = lax.axis_index("pcol")
    A, TILE, _ = panel.shape
    KF = factor.shape[0]
    CTD = strip.shape[0]
    I = factor.shape[1]
    KS = KF * C
    NR = rhs.shape[2]
    full = KS == R

    def target(row):
        return jnp.where(row == 0, KS, row) if full else row

    def has_row(row):
        return True if full else jnp.logical_and(row >= 1, row <= KS)

    def slot(row):
        return target(row) if full else jnp.minimum(row, KS)

    first = jnp.where(r == 0, KS // R, 0) if full else 0

    barrier = pltpu.get_barrier_semaphore()

    @pl.loop(1, C)
    def _(d):
        pl.semaphore_signal(barrier, inc=1, device_id={"pcol": lax.rem(c + d, C)}, device_id_type=MESH)

    @pl.loop(1, R)
    def _(d):
        pl.semaphore_signal(barrier, inc=1, device_id={"prow": lax.rem(r + d, R)}, device_id_type=MESH)

    pl.semaphore_wait(barrier, C - 1 + R - 1)

    def z_copy(kind, d, source, place):
        if kind < KF:
            src, dst = factor.at[kind, first], ftri.at[slot(r), kind * C + source]
        elif kind == KF:
            src, dst = panel, pan_all.at[pl.ds(source * A, A)]
        elif kind == KF + 1:
            src, dst = factor.at[:, pl.ds(place * A, A)], frow.at[:, source]
        else:
            src, dst = panel.at[KS // R % A], diag
        return pltpu.make_async_remote_copy(
            src_ref=src, dst_ref=dst, send_sem=z_send.at[kind, d - 1], recv_sem=z_recv.at[kind, d - 1],
            device_id={"pcol": place}, device_id_type=MESH,
        )

    def tiles_of(row):
        return target(row) if full else jnp.where(row <= KS, row, 0)

    def z_cond(kind, source):
        if kind == KF + 2:
            return jnp.logical_and(r == KS % R, source == KS // R // A)
        return kind * C + source < tiles_of(r) if kind < KF else True

    def z_start(kind):
        for d in range(1, C):
            when(z_cond(kind, c), lambda d=d: z_copy(kind, d, c, lax.rem(c + d, C)).start())

    def z_wait_send(kind):
        for d in range(1, C):
            when(z_cond(kind, c), lambda d=d: z_copy(kind, d, c, lax.rem(c + d, C)).wait_send())

    def z_wait_recv(kind):
        for d in range(1, C):
            source = lax.rem(c + C - d, C)
            when(z_cond(kind, source), lambda d=d, source=source: z_copy(kind, d, source, c).wait_recv())

    side = lax.rem(r, 2)
    sibling = r + 1 - 2 * side

    def wanted(s):
        return KS + 1 + s * C + c

    def p_place(kind, row):
        if kind == 0:
            return brow.at[jnp.minimum(row, KS - 1)]
        if kind == 1:
            return brow.at[KS]
        if kind == 2:
            return diag
        return col.at[kind - 3]

    def p_cond(kind, row):
        if kind == 0:
            return True if full else row < KS
        if kind <= 2:
            return row == KS % R
        return row == lax.rem(wanted(kind - 3), R)

    def p_copy(kind, row, place, sem):
        ref = p_place(kind, row)
        return pltpu.make_async_remote_copy(
            src_ref=ref, dst_ref=ref, send_sem=sem, recv_sem=p_recv.at[kind, row],
            device_id={"prow": place}, device_id_type=MESH,
        )

    def t_copy(j, row, place, sem):
        ref = ftri.at[slot(row), j]
        return pltpu.make_async_remote_copy(
            src_ref=ref, dst_ref=ref, send_sem=sem, recv_sem=p_recv.at[3 + CTD + j, row],
            device_id={"prow": place}, device_id_type=MESH,
        )

    def each(kinds, row, act, t_act):
        for kind in kinds:
            if kind == "tiles":
                def one(j, carry):
                    t_act(j)
                    return carry

                lax.fori_loop(0, tiles_of(row), one, 0)
            else:
                when(p_cond(kind, row), lambda kind=kind: act(kind))

    def p_own(kinds, finish):
        def go(copy):
            if finish:
                copy.wait_send()
            else:
                copy.start()

        @pl.loop(0, R // 2)
        def _(d):
            place = jnp.where(d == 0, sibling, lax.rem(r + 2 * d, R))
            each(
                kinds, r,
                lambda kind: go(p_copy(kind, r, place, p_send.at[kind, d])),
                lambda j: go(t_copy(j, r, place, p_send.at[3 + CTD + j, d])),
            )

    def p_pass(kinds):
        @pl.loop(1, R // 2)
        def _(d):
            row = lax.rem(r + R - 2 * d, R)

            def act(kind):
                p_copy(kind, row, sibling, f_send.at[kind, d]).wait_recv()
                p_copy(kind, row, sibling, f_send.at[kind, d]).start()

            def t_act(j):
                t_copy(j, row, sibling, f_send.at[3 + CTD + j, d]).wait_recv()
                t_copy(j, row, sibling, f_send.at[3 + CTD + j, d]).start()

            each(kinds, row, act, t_act)

    def p_pass_done(kinds):
        @pl.loop(1, R // 2)
        def _(d):
            row = lax.rem(r + R - 2 * d, R)
            each(
                kinds, row,
                lambda kind: p_copy(kind, row, sibling, f_send.at[kind, d]).wait_send(),
                lambda j: t_copy(j, row, sibling, f_send.at[3 + CTD + j, d]).wait_send(),
            )

    def p_rest(kinds):
        @pl.loop(0, R // 2)
        def _(d):
            row = 2 * d + 1 - side
            each(
                kinds, row,
                lambda kind: p_copy(kind, row, sibling, f_send.at[kind, 0]).wait_recv(),
                lambda j: t_copy(j, row, sibling, f_send.at[3 + CTD + j, 0]).wait_recv(),
            )

    z_start(KF + 2)
    for kind in range(KF):
        z_start(kind)

    z_start(KF + 1)
    z_start(KF)

    def keep_rhs():
        brow[jnp.minimum(r, KS - 1)] = rhs[0]

    when(p_cond(0, r), keep_rhs)

    @pl.when(p_cond(1, r))
    def _():
        brow[KS] = rhs[KS // R]

    p_own((0, 1), False)

    @pl.when(z_cond(KF + 2, c))
    def _():
        diag[...] = panel[KS // R % A]

    for s in range(KF):
        @pl.when(z_cond(s, c))
        def _(s=s):
            ftri[slot(r), s * C + c] = factor[s, first]

    z_wait_recv(KF + 2)
    p_own((2,), False)
    for kind in range(KF):
        z_wait_recv(kind)
    p_own(("tiles",), False)
    own = pltpu.make_async_copy(factor.at[:, pl.ds(c * A, A)], frow.at[:, c], local_sem)
    own.start()
    pan_all[pl.ds(c * A, A)] = panel[...]
    late = tuple(range(3, 3 + CTD))
    p_pass((2,))
    p_rest((2,))

    lanes = lax.broadcasted_iota(jnp.int32, (TILE, TILE), 1)
    rows = lax.broadcasted_iota(jnp.int32, (TILE, TILE), 0)
    tri[...] = diag[...]
    inv[...] = jnp.where(lanes == rows, 1.0, 0.0)

    def eliminate(k, carry):
        lane = lanes[0:1]
        row = tri[pl.ds(k, 1), :]
        whole = tri[...]
        pivot = jnp.sum(jnp.where(lane == k, row, 0.0), axis=1, keepdims=True)
        scale = 1.0 / jnp.sqrt(pivot)
        lrow = jnp.where(lane >= k, row * scale, 0.0)
        column = jnp.sum(jnp.where(lanes == k, whole, 0.0), axis=1, keepdims=True)
        lcol = jnp.where(rows[:, 0:1] > k, column * scale, 0.0)
        wrow = inv[pl.ds(k, 1), :] * scale
        tri[...] = whole - lcol * lrow
        inv[...] = inv[...] - lcol * wrow
        tri[pl.ds(k, 1), :] = lrow
        inv[pl.ds(k, 1), :] = wrow
        return carry

    lax.fori_loop(0, TILE, eliminate, 0)
    inv_t[...] = inv[...].T

    p_pass((0, 1, "tiles"))
    p_rest((0, 1, "tiles"))
    p_own((0, 1), True)
    p_pass_done((0, 1))

    def advance(t, carry):
        y[t] = dot(inv_diag[t], brow[t])

        def update(row, carry):
            brow[row] = brow[row] - dot(ftri[row, t], y[t])
            return carry

        return lax.fori_loop(t + 1, KS + 1, update, carry)

    lax.fori_loop(0, KS, advance, 0)
    panel_solution = dot(inv[...], brow[KS])

    scaled = dot(panel[...].reshape(A * TILE, TILE), inv_t[...])
    for a in range(A):
        tile = (c * A + a) * R + r
        panel_out[a] = jnp.where(tile > KS, scaled[a * TILE:(a + 1) * TILE], 0.0)
    brow[KS] = panel_solution

    z_wait_recv(KF + 1)
    own.wait()

    def a_copy(way, source, a):
        place = jnp.clip(c + (1 if way else -1), 0, C - 1)
        ref = forward.at[source * A + a]
        return pltpu.make_async_remote_copy(
            src_ref=ref, dst_ref=ref,
            send_sem=a_send.at[way, source, a], recv_sem=a_recv.at[source, a],
            device_id={"pcol": place}, device_id_type=MESH,
        )

    def finish(a, carry):
        tile = (c * A + a) * R + r
        total = rhs[c * A + a] - dot(panel_out[a], brow[KS])

        def reach(j, total):
            return total - dot(frow[j // C, lax.rem(j, C), a], y[j])

        total = lax.fori_loop(0, KS, reach, total, unroll=True)
        forward[c * A + a] = total

        @pl.when(tile < KS)
        def _():
            forward[c * A + a] = y[jnp.minimum(tile, KS - 1)]

        @pl.when(tile == KS)
        def _():
            forward[c * A + a] = brow[KS]
            panel_out[a] = tri[...].T

        @pl.when(c < C - 1)
        def _():
            a_copy(1, c, a).start()

        @pl.when(c > 0)
        def _():
            a_copy(0, c, a).start()

        return carry

    lax.fori_loop(0, A, finish, 0)

    z_wait_recv(KF)
    for s in range(CTD):
        @pl.when(p_cond(3 + s, r))
        def _(s=s):
            col[s] = pan_all[wanted(s) // R]

    p_own(late, False)
    p_pass(late)
    p_rest(late)
    p_own(late, True)
    p_pass_done(late)
    for s in range(CTD):
        col[s] = dot(col[s], inv_t[...]).T

    def strip_row(i, carry):
        tile = i * R + r
        scaled = jnp.where(tile > KS, dot(pan_all[i], inv_t[...]), 0.0)
        for s in range(CTD):
            strip_out[s, i] = strip[s, i] - dot(scaled, col[s])
        return carry

    steps = (C - 1) * A

    def hop(n, carry):
        lax.fori_loop(n * I // steps, (n + 1) * I // steps, strip_row, 0)
        far = n // A + 1
        a = lax.rem(n, A)

        @pl.when(c - far >= 0)
        def _():
            a_copy(1, c - far, a).wait_recv()

            @pl.when(c < C - 1)
            def _():
                a_copy(1, c - far, a).start()

        @pl.when(c + far < C)
        def _():
            a_copy(0, c + far, a).wait_recv()

            @pl.when(c > 0)
            def _():
                a_copy(0, c + far, a).start()

        return carry

    lax.fori_loop(0, steps, hop, 0)

    for kind in range(KF + 3):
        z_wait_send(kind)
    p_own((2, "tiles"), True)
    p_pass_done((2, "tiles"))

    def flush(n, carry):
        source = n // A
        a = lax.rem(n, A)

        @pl.when(jnp.logical_and(source <= c, c < C - 1))
        def _():
            a_copy(1, source, a).wait_send()

        @pl.when(jnp.logical_and(source >= c, c > 0))
        def _():
            a_copy(0, source, a).wait_send()

        return carry

    lax.fori_loop(0, C * A, flush, 0)


def per_device(panel, strip, factor, inv_diag, rhs):
    R = lax.axis_size("prow")
    C = lax.axis_size("pcol")
    A, TILE, _ = panel.shape
    I, _, CTD, _ = strip.shape
    KF = factor.shape[2]
    NR = rhs.shape[2]
    KS = KF * C
    assert KS <= R
    f32 = jnp.float32
    strip = jnp.transpose(strip, (2, 0, 1, 3))
    factor = jnp.transpose(factor, (2, 0, 1, 3))
    kinds = 3 + CTD + KS
    dma = pltpu.SemaphoreType.DMA
    panel_factor, new_strip, forward = pl.pallas_call(
        functools.partial(kernel, R, C),
        out_shape=(
            jax.ShapeDtypeStruct(panel.shape, f32),
            jax.ShapeDtypeStruct(strip.shape, f32),
            jax.ShapeDtypeStruct(rhs.shape, f32),
        ),
        in_specs=[pl.BlockSpec(memory_space=pltpu.VMEM)] * 5,
        out_specs=[pl.BlockSpec(memory_space=pltpu.VMEM)] * 3,
        scratch_shapes=[
            pltpu.VMEM((I, TILE, TILE), f32),
            pltpu.VMEM((TILE, TILE), f32),
            pltpu.VMEM((CTD, TILE, TILE), f32),
            pltpu.VMEM((KS + 1, KS, TILE, TILE), f32),
            pltpu.VMEM((KS + 1, TILE, NR), f32),
            pltpu.VMEM((KS, TILE, NR), f32),
            pltpu.VMEM((KF, C, A, TILE, TILE), f32),
            pltpu.VMEM((TILE, TILE), f32),
            pltpu.VMEM((TILE, TILE), f32),
            pltpu.VMEM((TILE, TILE), f32),
            dma((KF + 3, C - 1)),
            dma((KF + 3, C - 1)),
            dma((kinds, R // 2)),
            dma((kinds, R)),
            dma((kinds, R // 2)),
            dma((2, C, A)),
            dma((C, A)),
            dma,
        ],
        compiler_params=pltpu.CompilerParams(
            collective_id=0, has_side_effects=True, vmem_limit_bytes=56 << 20
        ),
    )(panel, strip, factor, inv_diag, rhs)
    return panel_factor, jnp.transpose(new_strip, (1, 2, 0, 3)), forward


def solution(mesh):
    in_specs = (
        P("pcol", "prow", None),
        P(None, "prow", None, "pcol"),
        P(None, "prow", None, "pcol"),
        P(),
        P(None, "prow", None),
    )
    out_specs = (P("pcol", "prow", None), P(None, "prow", None, "pcol"), P(None, "prow", None))
    return jax.shard_map(
        per_device, mesh=mesh, in_specs=in_specs, out_specs=out_specs, check_vma=False
    )
```

```python
import functools

import jax
import jax.numpy as jnp
from jax import lax
from jax.experimental import pallas as pl
from jax.experimental.pallas import tpu as pltpu
from jax.sharding import PartitionSpec as P

HIGHEST = lax.Precision.HIGHEST
MESH = pl.DeviceIdType.MESH


def dot(a, b):
    return jnp.dot(a, b, precision=HIGHEST, preferred_element_type=jnp.float32)


def when(cond, body):
    if cond is True:
        body()
    else:
        pl.when(cond)(body)


def kernel(
    R, C,
    panel, strip, factor, inv_diag, rhs,
    panel_out, strip_out, forward,
    pan_all, diag, col, ftri, brow, y, frow, tri, inv, inv_t,
    z_send, z_recv, p_send, p_recv, f_send, a_send, a_recv, local_sem,
):
    r = lax.axis_index("prow")
    c = lax.axis_index("pcol")
    A, TILE, _ = panel.shape
    KF = factor.shape[0]
    CTD = strip.shape[2]
    I = factor.shape[1]
    KS = KF * C
    NR = rhs.shape[2]
    full = KS == R

    def target(row):
        return jnp.where(row == 0, KS, row) if full else row

    def has_row(row):
        return True if full else jnp.logical_and(row >= 1, row <= KS)

    def slot(row):
        return target(row) if full else jnp.minimum(row, KS)

    first = jnp.where(r == 0, KS // R, 0) if full else 0

    barrier = pltpu.get_barrier_semaphore()

    @pl.loop(1, C)
    def _(d):
        pl.semaphore_signal(barrier, inc=1, device_id={"pcol": lax.rem(c + d, C)}, device_id_type=MESH)

    @pl.loop(1, R)
    def _(d):
        pl.semaphore_signal(barrier, inc=1, device_id={"prow": lax.rem(r + d, R)}, device_id_type=MESH)

    pl.semaphore_wait(barrier, C - 1 + R - 1)

    def z_copy(kind, d, source, place):
        if kind < KF:
            src, dst = factor.at[kind, first], ftri.at[slot(r), kind * C + source]
        elif kind == KF:
            src, dst = panel, pan_all.at[pl.ds(source * A, A)]
        elif kind == KF + 1:
            src, dst = factor.at[:, pl.ds(place * A, A)], frow.at[:, source]
        else:
            src, dst = panel.at[KS // R % A], diag
        return pltpu.make_async_remote_copy(
            src_ref=src, dst_ref=dst, send_sem=z_send.at[kind, d - 1], recv_sem=z_recv.at[kind, d - 1],
            device_id={"pcol": place}, device_id_type=MESH,
        )

    def tiles_of(row):
        return target(row) if full else jnp.where(row <= KS, row, 0)

    def z_cond(kind, source):
        if kind == KF + 2:
            return jnp.logical_and(r == KS % R, source == KS // R // A)
        return kind * C + source < tiles_of(r) if kind < KF else True

    def z_start(kind):
        for d in range(1, C):
            when(z_cond(kind, c), lambda d=d: z_copy(kind, d, c, lax.rem(c + d, C)).start())

    def z_wait_send(kind):
        for d in range(1, C):
            when(z_cond(kind, c), lambda d=d: z_copy(kind, d, c, lax.rem(c + d, C)).wait_send())

    def z_wait_recv(kind):
        for d in range(1, C):
            source = lax.rem(c + C - d, C)
            when(z_cond(kind, source), lambda d=d, source=source: z_copy(kind, d, source, c).wait_recv())

    side = lax.rem(r, 2)
    sibling = r + 1 - 2 * side

    def wanted(s):
        return KS + 1 + s * C + c

    def p_place(kind, row):
        if kind == 0:
            return brow.at[jnp.minimum(row, KS - 1)]
        if kind == 1:
            return brow.at[KS]
        if kind == 2:
            return diag
        return col.at[kind - 3]

    def p_cond(kind, row):
        if kind == 0:
            return True if full else row < KS
        if kind <= 2:
            return row == KS % R
        return row == lax.rem(wanted(kind - 3), R)

    def p_copy(kind, row, place, sem):
        ref = p_place(kind, row)
        return pltpu.make_async_remote_copy(
            src_ref=ref, dst_ref=ref, send_sem=sem, recv_sem=p_recv.at[kind, row],
            device_id={"prow": place}, device_id_type=MESH,
        )

    def t_copy(j, row, place, sem):
        ref = ftri.at[slot(row), j]
        return pltpu.make_async_remote_copy(
            src_ref=ref, dst_ref=ref, send_sem=sem, recv_sem=p_recv.at[3 + CTD + j, row],
            device_id={"prow": place}, device_id_type=MESH,
        )

    def each(kinds, row, act, t_act):
        for kind in kinds:
            if kind == "tiles":
                def one(j, carry):
                    t_act(j)
                    return carry

                lax.fori_loop(0, tiles_of(row), one, 0)
            else:
                when(p_cond(kind, row), lambda kind=kind: act(kind))

    def p_own(kinds, finish):
        def go(copy):
            if finish:
                copy.wait_send()
            else:
                copy.start()

        @pl.loop(0, R // 2)
        def _(d):
            place = jnp.where(d == 0, sibling, lax.rem(r + 2 * d, R))
            each(
                kinds, r,
                lambda kind: go(p_copy(kind, r, place, p_send.at[kind, d])),
                lambda j: go(t_copy(j, r, place, p_send.at[3 + CTD + j, d])),
            )

    def p_pass(kinds):
        @pl.loop(1, R // 2)
        def _(d):
            row = lax.rem(r + R - 2 * d, R)

            def act(kind):
                p_copy(kind, row, sibling, f_send.at[kind, d]).wait_recv()
                p_copy(kind, row, sibling, f_send.at[kind, d]).start()

            def t_act(j):
                t_copy(j, row, sibling, f_send.at[3 + CTD + j, d]).wait_recv()
                t_copy(j, row, sibling, f_send.at[3 + CTD + j, d]).start()

            each(kinds, row, act, t_act)

    def p_pass_done(kinds):
        @pl.loop(1, R // 2)
        def _(d):
            row = lax.rem(r + R - 2 * d, R)
            each(
                kinds, row,
                lambda kind: p_copy(kind, row, sibling, f_send.at[kind, d]).wait_send(),
                lambda j: t_copy(j, row, sibling, f_send.at[3 + CTD + j, d]).wait_send(),
            )

    def p_rest(kinds):
        @pl.loop(0, R // 2)
        def _(d):
            row = 2 * d + 1 - side
            each(
                kinds, row,
                lambda kind: p_copy(kind, row, sibling, f_send.at[kind, 0]).wait_recv(),
                lambda j: t_copy(j, row, sibling, f_send.at[3 + CTD + j, 0]).wait_recv(),
            )

    z_start(KF + 2)
    for kind in range(KF):
        z_start(kind)

    z_start(KF + 1)
    z_start(KF)

    def keep_rhs():
        brow[jnp.minimum(r, KS - 1)] = rhs[0]

    when(p_cond(0, r), keep_rhs)

    @pl.when(p_cond(1, r))
    def _():
        brow[KS] = rhs[KS // R]

    p_own((0, 1), False)

    @pl.when(z_cond(KF + 2, c))
    def _():
        diag[...] = panel[KS // R % A]

    for s in range(KF):
        @pl.when(z_cond(s, c))
        def _(s=s):
            ftri[slot(r), s * C + c] = factor[s, first]

    z_wait_recv(KF + 2)
    p_own((2,), False)
    for kind in range(KF):
        z_wait_recv(kind)
    p_own(("tiles",), False)
    own = pltpu.make_async_copy(factor.at[:, pl.ds(c * A, A)], frow.at[:, c], local_sem)
    own.start()
    pan_all[pl.ds(c * A, A)] = panel[...]
    late = tuple(range(3, 3 + CTD))
    p_pass((2,))
    p_rest((2,))

    lanes = lax.broadcasted_iota(jnp.int32, (TILE, TILE), 1)
    rows = lax.broadcasted_iota(jnp.int32, (TILE, TILE), 0)
    tri[...] = diag[...]
    inv[...] = jnp.where(lanes == rows, 1.0, 0.0)

    def eliminate(k, carry):
        lane = lanes[0:1]
        row = tri[pl.ds(k, 1), :]
        whole = tri[...]
        pivot = jnp.sum(jnp.where(lane == k, row, 0.0), axis=1, keepdims=True)
        scale = 1.0 / jnp.sqrt(pivot)
        lrow = jnp.where(lane >= k, row * scale, 0.0)
        column = jnp.sum(jnp.where(lanes == k, whole, 0.0), axis=1, keepdims=True)
        lcol = jnp.where(rows[:, 0:1] > k, column * scale, 0.0)
        wrow = inv[pl.ds(k, 1), :] * scale
        tri[...] = whole - lcol * lrow
        inv[...] = inv[...] - lcol * wrow
        tri[pl.ds(k, 1), :] = lrow
        inv[pl.ds(k, 1), :] = wrow
        return carry

    lax.fori_loop(0, TILE, eliminate, 0)
    inv_t[...] = inv[...].T

    p_pass((0, 1, "tiles"))
    p_rest((0, 1, "tiles"))
    p_own((0, 1), True)
    p_pass_done((0, 1))

    def advance(t, carry):
        y[t] = dot(inv_diag[t], brow[t])

        def update(row, carry):
            brow[row] = brow[row] - dot(ftri[row, t], y[t])
            return carry

        return lax.fori_loop(t + 1, KS + 1, update, carry)

    lax.fori_loop(0, KS, advance, 0)
    panel_solution = dot(inv[...], brow[KS])

    scaled = dot(panel[...].reshape(A * TILE, TILE), inv_t[...])
    for a in range(A):
        tile = (c * A + a) * R + r
        panel_out[a] = jnp.where(tile > KS, scaled[a * TILE:(a + 1) * TILE], 0.0)
    brow[KS] = panel_solution

    z_wait_recv(KF + 1)
    own.wait()

    def a_copy(way, source, a):
        place = jnp.clip(c + (1 if way else -1), 0, C - 1)
        ref = forward.at[source * A + a]
        return pltpu.make_async_remote_copy(
            src_ref=ref, dst_ref=ref,
            send_sem=a_send.at[way, source, a], recv_sem=a_recv.at[source, a],
            device_id={"pcol": place}, device_id_type=MESH,
        )

    def finish(a, carry):
        tile = (c * A + a) * R + r
        total = rhs[c * A + a] - dot(panel_out[a], brow[KS])

        def reach(j, total):
            return total - dot(frow[j // C, lax.rem(j, C), a], y[j])

        total = lax.fori_loop(0, KS, reach, total, unroll=True)
        forward[c * A + a] = total

        @pl.when(tile < KS)
        def _():
            forward[c * A + a] = y[jnp.minimum(tile, KS - 1)]

        @pl.when(tile == KS)
        def _():
            forward[c * A + a] = brow[KS]
            panel_out[a] = tri[...].T

        @pl.when(c < C - 1)
        def _():
            a_copy(1, c, a).start()

        @pl.when(c > 0)
        def _():
            a_copy(0, c, a).start()

        return carry

    lax.fori_loop(0, A, finish, 0)

    z_wait_recv(KF)
    for s in range(CTD):
        @pl.when(p_cond(3 + s, r))
        def _(s=s):
            col[s] = pan_all[wanted(s) // R]

    p_own(late, False)
    p_pass(late)
    p_rest(late)
    p_own(late, True)
    p_pass_done(late)
    for s in range(CTD):
        col[s] = dot(col[s], inv_t[...]).T

    def strip_row(i, carry):
        tile = i * R + r
        scaled = jnp.where(tile > KS, dot(pan_all[i], inv_t[...]), 0.0)
        for s in range(CTD):
            strip_out[i, :, s, :] = strip[i, :, s, :] - dot(scaled, col[s])
        return carry

    steps = (C - 1) * A

    def hop(n, carry):
        lax.fori_loop(n * I // steps, (n + 1) * I // steps, strip_row, 0)
        far = n // A + 1
        a = lax.rem(n, A)

        @pl.when(c - far >= 0)
        def _():
            a_copy(1, c - far, a).wait_recv()

            @pl.when(c < C - 1)
            def _():
                a_copy(1, c - far, a).start()

        @pl.when(c + far < C)
        def _():
            a_copy(0, c + far, a).wait_recv()

            @pl.when(c > 0)
            def _():
                a_copy(0, c + far, a).start()

        return carry

    lax.fori_loop(0, steps, hop, 0)

    for kind in range(KF + 3):
        z_wait_send(kind)
    p_own((2, "tiles"), True)
    p_pass_done((2, "tiles"))

    def flush(n, carry):
        source = n // A
        a = lax.rem(n, A)

        @pl.when(jnp.logical_and(source <= c, c < C - 1))
        def _():
            a_copy(1, source, a).wait_send()

        @pl.when(jnp.logical_and(source >= c, c > 0))
        def _():
            a_copy(0, source, a).wait_send()

        return carry

    lax.fori_loop(0, C * A, flush, 0)


def per_device(panel, strip, factor, inv_diag, rhs):
    R = lax.axis_size("prow")
    C = lax.axis_size("pcol")
    A, TILE, _ = panel.shape
    I, _, CTD, _ = strip.shape
    KF = factor.shape[2]
    NR = rhs.shape[2]
    KS = KF * C
    assert KS <= R
    f32 = jnp.float32
    factor = jnp.transpose(factor, (2, 0, 1, 3))
    kinds = 3 + CTD + KS
    dma = pltpu.SemaphoreType.DMA
    panel_factor, new_strip, forward = pl.pallas_call(
        functools.partial(kernel, R, C),
        out_shape=(
            jax.ShapeDtypeStruct(panel.shape, f32),
            jax.ShapeDtypeStruct(strip.shape, f32),
            jax.ShapeDtypeStruct(rhs.shape, f32),
        ),
        in_specs=[pl.BlockSpec(memory_space=pltpu.VMEM)] * 5,
        out_specs=[pl.BlockSpec(memory_space=pltpu.VMEM)] * 3,
        scratch_shapes=[
            pltpu.VMEM((I, TILE, TILE), f32),
            pltpu.VMEM((TILE, TILE), f32),
            pltpu.VMEM((CTD, TILE, TILE), f32),
            pltpu.VMEM((KS + 1, KS, TILE, TILE), f32),
            pltpu.VMEM((KS + 1, TILE, NR), f32),
            pltpu.VMEM((KS, TILE, NR), f32),
            pltpu.VMEM((KF, C, A, TILE, TILE), f32),
            pltpu.VMEM((TILE, TILE), f32),
            pltpu.VMEM((TILE, TILE), f32),
            pltpu.VMEM((TILE, TILE), f32),
            dma((KF + 3, C - 1)),
            dma((KF + 3, C - 1)),
            dma((kinds, R // 2)),
            dma((kinds, R)),
            dma((kinds, R // 2)),
            dma((2, C, A)),
            dma((C, A)),
            dma,
        ],
        compiler_params=pltpu.CompilerParams(
            collective_id=0, has_side_effects=True, vmem_limit_bytes=56 << 20
        ),
    )(panel, strip, factor, inv_diag, rhs)
    return panel_factor, new_strip, forward


def solution(mesh):
    in_specs = (
        P("pcol", "prow", None),
        P(None, "prow", None, "pcol"),
        P(None, "prow", None, "pcol"),
        P(),
        P(None, "prow", None),
    )
    out_specs = (P("pcol", "prow", None), P(None, "prow", None, "pcol"), P(None, "prow", None))
    return jax.shard_map(
        per_device, mesh=mesh, in_specs=in_specs, out_specs=out_specs, check_vma=False
    )
```
